1024 devices in a mesh: expert: 64 (over z, x), tensor: 16 (over y, core).
Axes of the slice: x: 8, y: 8, z: 8, core: 2. Of those that a mesh axis runs over, the one named last changes fastest.
Arguments:
- hidden: bfloat16 [64, 1536, 2048], P('expert'), may hold values from -6 to 6
- down_weight: bfloat16 [64, 2048, 7168], P('expert', None, 'tensor'), may hold values from -0.125 to 0.125
- expert_ids: int32 [8192, 8], P('expert'), may hold values from 0 to 63, as said below
- gate_weights: float32 [8192, 8], P('expert'), may hold values from 0.1 to 0.6
- residual: bfloat16 [8192, 7168], P('expert', 'tensor'), may hold values from -36 to 36
- norm_gain: float32 [7168], replicated, may hold values from 0.1 to 1.9
- proj_weight: bfloat16 [7168, 2112], P(None, 'tensor'), may hold values from -0.0625 to 0.0625
Outputs:
- stream: bfloat16 [8192, 7168], P('expert', 'tensor')
- latents: bfloat16 [8192, 2112], P('expert', 'tensor')
The draws below stay inside these ranges and needn't reach their ends.
Inputs may be any that keep to these rules, and one draw needn't show every extreme that they name: `expert_ids`: experts 4 g to 4 g + 3 form node group g. Each token names 8 different experts, two in each of exactly 4 node groups. Within each aligned block of 128 tokens no expert is named by more than 24 tokens and no node group is used by more than 48 tokens; in every block some node group is used by exactly 48 tokens and each of its experts is named by exactly 24.
All inputs are finite; a program needn't handle non-finite values.
Results may differ from the reference program's by a relative error of at most 0.014.
Values may be sent and summed in bfloat16 or wider, within the bound.
A program may use at most 64 MiB of HBM per device.

```python
import jax
import jax.numpy as jnp
from jax import lax

D = 7168
FF = 2048
TOPK = 8
NODE_SIZE = 4
GROUP_PICK = 4
EXPERTS = 64
NODE_GROUPS = 16
TOK_GRP = 128
TOKENS = 8192
CAP = 24
GROUP_SLOTS = 1536
LATENT = 2112
N_EXPERT = 64


def draw_residual(key, part):
    first_key, second_key = jax.random.split(jax.random.fold_in(key, 11))
    column_scale = 0.5 + jnp.arange(D, dtype=jnp.float32) / D
    values = jnp.clip(jax.random.normal(first_key, (TOKENS, D), jnp.float32), -6.0, 6.0)
    row_scale = jnp.exp(jax.random.uniform(second_key, (TOKENS, 1), jnp.float32, 0.0, 1.38))
    return (values * column_scale * row_scale).astype(jnp.bfloat16)


def permutations(key, count, length):
    keys = jax.random.split(key, count)
    return jax.vmap(lambda single: jax.random.permutation(single, length))(keys).astype(jnp.int32)


def draw_expert_ids(key, part):
    keys = jax.random.split(jax.random.fold_in(key, 23), 5)
    block_count = TOKENS // TOK_GRP
    group_count = EXPERTS // NODE_SIZE
    entry_count = GROUP_PICK * TOK_GRP
    top_load = 2 * CAP
    other_count = group_count - 1
    remainder = entry_count - top_load
    fill_base = remainder // other_count
    fill_extra = remainder % other_count
    spread_most = max(0, min(top_load - fill_base - 1, fill_base))
    pair_count = other_count // 2
    loads = jnp.broadcast_to(fill_base + (jnp.arange(other_count, dtype=jnp.int32) < fill_extra).astype(jnp.int32), (block_count, other_count))
    if pair_count > 0:
        moved = jax.random.randint(keys[0], (block_count, pair_count), 0, spread_most + 1).astype(jnp.int32)
        loads = loads.at[:, 0:2 * pair_count:2].add(moved)
        loads = loads.at[:, 1:2 * pair_count:2].add(-moved)
    loads = jnp.concatenate([jnp.full((block_count, 1), top_load, jnp.int32), loads], axis=1)
    group_order = permutations(keys[1], block_count, group_count)
    ends = jnp.cumsum(loads, axis=1)
    starts = ends - loads
    position = jnp.arange(entry_count, dtype=jnp.int32)
    rank_of = jnp.sum((ends[:, None, :] <= position[None, :, None]).astype(jnp.int32), axis=2)
    within = position[None, :] - jnp.take_along_axis(starts, rank_of, axis=1)
    group_of = jnp.take_along_axis(group_order, rank_of, axis=1)
    first_table = jnp.array([0, 2, 0, 1, 0, 1], jnp.int32)
    second_table = jnp.array([1, 3, 2, 3, 3, 2], jnp.int32)
    first_member = first_table[within % 6]
    second_member = second_table[within % 6]
    member_order = permutations(keys[2], block_count * group_count, NODE_SIZE).reshape(block_count, group_count * NODE_SIZE)
    first_expert = group_of * NODE_SIZE + jnp.take_along_axis(member_order, group_of * NODE_SIZE + first_member, axis=1)
    second_expert = group_of * NODE_SIZE + jnp.take_along_axis(member_order, group_of * NODE_SIZE + second_member, axis=1)
    chosen = jnp.stack([first_expert, second_expert], axis=2).reshape(block_count, GROUP_PICK, TOK_GRP, 2)
    chosen = jnp.transpose(chosen, (0, 2, 1, 3)).reshape(block_count, TOK_GRP, TOPK)
    token_order = permutations(keys[3], block_count, TOK_GRP)
    chosen = jnp.take_along_axis(chosen, token_order[:, :, None], axis=1)
    column_order = permutations(keys[4], block_count * TOK_GRP, TOPK).reshape(block_count, TOK_GRP, TOPK)
    chosen = jnp.take_along_axis(chosen, column_order, axis=2)
    return chosen.reshape(TOKENS, TOPK).astype(jnp.int32)


def levels(stream_key, extent, cuts, low, largest):
    def one(dim, shards_of):
        draws = jax.random.uniform(jax.random.fold_in(jax.random.fold_in(stream_key, 6), dim), (shards_of,), jnp.float32, low / len(cuts), largest / len(cuts))
        return jnp.repeat(jnp.exp(draws), extent[dim] // shards_of).reshape((-1,) + (1,) * (len(extent) - dim - 1))

    loudness = one(*cuts[0])
    for cut in cuts[1:]:
        loudness = loudness * one(*cut)
    return loudness


def normal_values(rng, extent, scale, reach, cuts=(), held_as=jnp.bfloat16):
    level = levels(rng, extent, cuts, -0.22, 0.18) if cuts else 1.0
    values = jax.random.normal(rng, extent, jnp.float32) * scale * level
    return jnp.minimum(jnp.maximum(values, -reach), reach).astype(held_as)


def setup_inputs(seed: int = 0) -> dict:
    seeds = jax.random.split(jax.random.key(seed), 8)
    hidden = normal_values(seeds[0], (EXPERTS, GROUP_SLOTS, FF), 1.0, 6.0, ((0, 64),))
    down_weight = normal_values(seeds[1], (EXPERTS, FF, D), FF ** -0.5, 0.125, ((0, 64), (2, 16)))
    expert_ids = draw_expert_ids(jax.random.fold_in(seeds[7], 71), 0)
    gate_weights = jnp.clip(0.1 + 0.5 * jax.random.uniform(seeds[3], (TOKENS, TOPK), jnp.float32) ** levels(seeds[3], (TOKENS, TOPK), ((0, 64),), -0.2, 0.2), 0.1, 0.6)
    residual = draw_residual(jax.random.fold_in(seeds[7], 71), 0)
    norm_gain = jnp.clip(1.0 + 0.18 * jax.random.normal(seeds[5], (D,), jnp.float32), 0.1, 1.9)
    proj_weight = normal_values(seeds[6], (D, LATENT), D ** -0.5, 0.0625, ((1, 16),))
    return {"hidden": hidden, "down_weight": down_weight, "expert_ids": expert_ids, "gate_weights": gate_weights, "residual": residual, "norm_gain": norm_gain, "proj_weight": proj_weight}


epsilon = 1e-06

def reference(hidden, down_weight, expert_ids, gate_weights, residual, norm_gain, proj_weight):
    groups = expert_ids.reshape(N_EXPERT, TOK_GRP, TOPK)
    expert_range = jnp.arange(EXPERTS, dtype=jnp.int32)
    counts = lax.optimization_barrier(jnp.sum((groups[:, :, :, None] == expert_range).astype(jnp.int32), axis=2))
    before = jnp.cumsum(counts, axis=1) - counts
    slots = jnp.take_along_axis(before, groups, axis=2).reshape(TOKENS, TOPK).astype(jnp.int32)
    owner_base = jnp.arange(TOKENS, dtype=jnp.int32) // TOK_GRP * CAP
    slot_rows = (owner_base[:, None] + slots).astype(jnp.int32)

    def add_group(summed, group):

        def add_expert(partial_value, member):
            expert = (group * NODE_SIZE + member).astype(jnp.int32)
            product = jnp.dot(hidden[expert], down_weight[expert], preferred_element_type=jnp.float32).astype(jnp.bfloat16)
            chosen = expert_ids == expert
            weighting = lax.optimization_barrier(jnp.sum(jnp.where(chosen, gate_weights, jnp.zeros_like(gate_weights)), axis=1))
            row_index = lax.optimization_barrier(jnp.sum(jnp.where(chosen, slot_rows, jnp.zeros_like(slot_rows)), axis=1)).astype(jnp.int32)
            addition = weighting[:, None] * product[row_index].astype(jnp.float32)
            return (partial_value + addition, None)
        partial_value, _ = lax.scan(add_expert, jnp.zeros((TOKENS, D), jnp.float32), jnp.arange(NODE_SIZE, dtype=jnp.int32))
        rounded = lax.optimization_barrier(partial_value.astype(jnp.bfloat16))
        return (summed + rounded.astype(jnp.float32), None)
    summed, _ = lax.scan(add_group, residual.astype(jnp.float32), jnp.arange(NODE_GROUPS, dtype=jnp.int32))
    stream = summed.astype(jnp.bfloat16)
    stream_wide = stream.astype(jnp.float32)
    energy = lax.optimization_barrier(jnp.mean(stream_wide * stream_wide, axis=1))
    normed = (stream_wide * norm_gain).astype(jnp.bfloat16)
    projected = jnp.dot(normed, proj_weight, preferred_element_type=jnp.float32)
    latents = (projected * lax.rsqrt(energy + epsilon)[:, None]).astype(jnp.bfloat16)
    return (stream, latents)
```

```python
import jax
import jax.numpy as jnp
from jax import lax
from jax.experimental import pallas as pl
from jax.experimental.pallas import tpu as pltpu
from jax.sharding import PartitionSpec as P

MESH = pl.DeviceIdType.MESH
F32 = jnp.float32
BF16 = jnp.bfloat16

D = 7168
SIDE = 8
CAP = 24
TOKENS = 128
ROWS = SIDE * CAP
PAIR = 2 * CAP
COLS = 448
LATENT = 132
HOPS = (1, 7, 2, 6, 3, 5, 4)
X_FIRST = (True, False, True, False)
epsilon = 1e-06


def kernel(
    hidden_ref, down_ref, proj_ref, meta_ref, residual_ref, gain_ref,
    stream_ref, latents_ref,
    hid, wts, wts2, proj, meta_x, meta_z, gate_x, gate_z,
    out, out3, got, got3, part, part3, came, came3, all_, all3, acc, square,
    load_sem, hid_sem, meta_ss, meta_rs, one_ss, one_rs, two_ss, two_rs, ring_ss, ring_rs,
):
    expert = lax.axis_index("expert")
    tensor = lax.axis_index("tensor")
    z, x = expert // SIDE, expert % SIDE
    y, core = tensor // 2, tensor % 2
    lane = lax.broadcasted_iota(jnp.int32, (1, 128), 1)
    low = lane < 64

    load_w = pltpu.make_async_copy(down_ref, wts, load_sem.at[0])
    load_w.start()

    def load_hidden(tile):
        rows = pl.ds(pl.multiple_of(tile * 2 * ROWS, 2 * ROWS), 2 * ROWS)
        return pltpu.make_async_copy(hidden_ref.at[rows], hid.at[rows], hid_sem.at[tile])

    for tile in range(4):
        load_hidden(tile).start()
    load_p = pltpu.make_async_copy(proj_ref, proj, load_sem.at[1])
    load_p.start()

    def along_x(index):
        return {"expert": z * SIDE + index, "tensor": tensor}

    def along_z(index):
        return {"expert": index * SIDE + x, "tensor": tensor}

    def along_y(index):
        return {"expert": expert, "tensor": index * 2 + core}

    partner = {"expert": expert, "tensor": y * 2 + 1 - core}
    up, down = (y + 1) % SIDE, (y + SIDE - 1) % SIDE

    barrier = pltpu.get_barrier_semaphore()
    for hop in HOPS:
        pl.semaphore_signal(barrier, inc=1, device_id=along_x((x + hop) % SIDE), device_id_type=MESH)
        pl.semaphore_signal(barrier, inc=1, device_id=along_z((z + hop) % SIDE), device_id_type=MESH)
    pl.semaphore_signal(barrier, inc=1, device_id=along_y(up), device_id_type=MESH)
    pl.semaphore_signal(barrier, inc=1, device_id=along_y(down), device_id_type=MESH)
    pl.semaphore_signal(barrier, inc=1, device_id=partner, device_id_type=MESH)
    pl.semaphore_wait(barrier, 17)

    def remote(source, target, send_sem, recv_sem, device):
        return pltpu.make_async_remote_copy(
            src_ref=source, dst_ref=target, send_sem=send_sem, recv_sem=recv_sem,
            device_id=device, device_id_type=MESH,
        )

    def meta_copies(hop):
        to_z, to_x = (z + hop) % SIDE, (x + hop) % SIDE
        return (
            remote(meta_ref, meta_x.at[z], meta_ss.at[0, hop], meta_rs.at[0, z], along_z(to_z)),
            remote(meta_ref, meta_z.at[x], meta_ss.at[1, hop], meta_rs.at[1, x], along_x(to_x)),
        )

    for hop in HOPS:
        for copy in meta_copies(hop):
            copy.start()
    meta_x[z] = meta_ref[...]
    meta_z[x] = meta_ref[...]

    def buffers(chunk):
        if chunk < 3:
            return out.at[chunk], got.at[chunk], part.at[chunk], came.at[chunk], all_.at[chunk]
        return out3, got3, part3, came3, all3

    def first_axis(chunk):
        return (x, along_x) if X_FIRST[chunk] else (z, along_z)

    def second_axis(chunk):
        return (z, along_z) if X_FIRST[chunk] else (x, along_x)

    def one_copy(chunk, hop):
        source, target = buffers(chunk)[:2]
        me, along = first_axis(chunk)
        to = (me + hop) % SIDE
        return remote(source.at[to], target.at[me], one_ss.at[chunk, hop], one_rs.at[chunk, me], along(to))

    def one_arrival(chunk, hop):
        source, target = buffers(chunk)[:2]
        me, along = first_axis(chunk)
        origin = (me + hop) % SIDE
        return remote(source.at[me], target.at[origin], one_ss.at[chunk, hop], one_rs.at[chunk, origin], along(origin))

    def two_copy(chunk, hop):
        source, target = buffers(chunk)[2:4]
        me, along = second_axis(chunk)
        to = (me + hop) % SIDE
        return remote(source.at[to], target.at[me], two_ss.at[chunk, hop], two_rs.at[chunk, me], along(to))

    def two_arrival(chunk, hop):
        source, target = buffers(chunk)[2:4]
        me, along = second_axis(chunk)
        origin = (me + hop) % SIDE
        return remote(source.at[me], target.at[origin], two_ss.at[chunk, hop], two_rs.at[chunk, origin], along(origin))

    def keep_own(chunk):
        source, target = buffers(chunk)[:2]
        me, _ = first_axis(chunk)
        target[me] = source[me]

    def tile_rows(tile):
        return pl.ds(pl.multiple_of(tile * 2 * ROWS, 2 * ROWS), 2 * ROWS)

    def store_x_first(chunk, tile, value):
        rows = pl.ds(pl.multiple_of(tile * PAIR, 16), PAIR)
        for j in range(SIDE):
            both = jnp.concatenate(
                [value[j * CAP:(j + 1) * CAP], value[ROWS + j * CAP:ROWS + (j + 1) * CAP]], axis=0
            )
            out[chunk, j, rows, :] = both.astype(BF16)

    load_w.wait()

    def first_half(tile, carry):
        load_hidden(tile).wait()
        value = jnp.dot(hid[tile_rows(tile), :], wts[:, 0:256], preferred_element_type=F32)
        store_x_first(0, tile, value[:, :128])
        for q in range(2):
            out[1, 2 * tile + q] = value[q * ROWS:(q + 1) * ROWS, 128:].astype(BF16)
        return carry

    lax.fori_loop(0, 4, first_half, 0)
    for hop in HOPS:
        one_copy(0, hop).start()
        one_copy(1, hop).start()
    keep_own(0)
    keep_own(1)

    wts2[:, :128] = wts[:, 256:384]
    last = wts[:, 384:448]
    wts2[:, 128:] = jnp.concatenate([last, last], axis=1)

    def second_half(tile, carry):
        value = jnp.dot(hid[tile_rows(tile), :], wts2[...], preferred_element_type=F32)
        store_x_first(2, tile, value[:, :128])
        for q in range(2):
            wide = value[q * ROWS:(q + 1) * ROWS, 128:]
            out3[2 * tile + q] = jnp.where(low, wide[:ROWS // 2], wide[ROWS // 2:]).astype(BF16)
        return carry

    lax.fori_loop(0, 4, second_half, 0)
    for hop in HOPS:
        one_copy(2, hop).start()
        one_copy(3, hop).start()
    keep_own(2)
    keep_own(3)

    for hop in HOPS:
        to_z, to_x = (z + hop) % SIDE, (x + hop) % SIDE
        remote(meta_ref, meta_x.at[to_z], meta_ss.at[0, hop], meta_rs.at[0, to_z], along_z(to_z)).wait_recv()
        remote(meta_ref, meta_z.at[to_x], meta_ss.at[1, hop], meta_rs.at[1, to_x], along_x(to_x)).wait_recv()
    earlier = (
        lax.broadcasted_iota(jnp.int32, (128, 128), 0) < lax.broadcasted_iota(jnp.int32, (128, 128), 1)
    ).astype(BF16)
    place = lax.broadcasted_iota(jnp.int32, (CAP, 128), 0).astype(F32)
    nothing = jnp.zeros((CAP, 128), F32)

    def build(meta, gates, base, step):
        def pair(p, carry):
            blocks = []
            for q in range(2):
                info = meta[2 * p + q]
                ids, weights = info[:8], info[8:]
                used, gate = [], []
                for a in range(SIDE):
                    match = ids == (base + a * step).astype(F32)
                    used.append(jnp.sum(jnp.where(match, 1.0, 0.0), axis=0, keepdims=True))
                    gate.append(jnp.sum(jnp.where(match, weights, 0.0), axis=0, keepdims=True))
                chosen = jnp.concatenate(used, axis=0)
                before = jnp.dot(chosen.astype(BF16), earlier, preferred_element_type=F32)
                where = jnp.where(chosen > 0.5, before, -1.0)
                blocks.append([jnp.where(where[a:a + 1] == place, gate[a], 0.0) for a in range(SIDE)])
            rows = []
            for a in range(SIDE):
                rows.append(jnp.concatenate([blocks[0][a], nothing], axis=1))
                rows.append(jnp.concatenate([nothing, blocks[1][a]], axis=1))
            gates[p] = jnp.concatenate(rows, axis=0).T.astype(BF16)
            return carry

        lax.fori_loop(0, 4, pair, 0)

    build(meta_x, gate_x, z * SIDE, jnp.int32(1))
    build(meta_z, gate_z, x, jnp.int32(SIDE))

    def merge(chunk):
        for hop in HOPS:
            one_arrival(chunk, hop).wait_recv()
        gates = gate_x if X_FIRST[chunk] else gate_z

        def pair(p, carry):
            rows = pl.ds(pl.multiple_of(p * PAIR, 16), PAIR)
            met = jnp.concatenate([got[chunk, a, rows, :] for a in range(SIDE)], axis=0)
            both = jnp.dot(gates[p], met, preferred_element_type=F32).astype(BF16)
            part[chunk, 2 * p] = both[:TOKENS]
            part[chunk, 2 * p + 1] = both[TOKENS:]
            return carry

        lax.fori_loop(0, 4, pair, 0)
        for hop in HOPS:
            two_copy(chunk, hop).start()

    def merge_last():
        for hop in HOPS:
            one_arrival(3, hop).wait_recv()
        for p in range(2):
            met = jnp.concatenate([got3[a, p * PAIR:(p + 1) * PAIR, :] for a in range(SIDE)], axis=0)
            left = jnp.dot(gate_z[p], met, preferred_element_type=F32)
            right = jnp.dot(gate_z[p + 2], met, preferred_element_type=F32)
            for q in range(2):
                value = left[q * TOKENS:(q + 1) * TOKENS]
                part3[2 * p + q] = jnp.where(low, value[:64], pltpu.roll(value[64:], 64, 1)).astype(BF16)
                value = right[q * TOKENS:(q + 1) * TOKENS]
                part3[2 * p + 4 + q] = jnp.where(low, pltpu.roll(value[:64], 64, 1), value[64:]).astype(BF16)
        for hop in HOPS:
            two_copy(3, hop).start()

    def ring_copy(chunk, source_y, device, number):
        block = buffers(chunk)[4].at[source_y * 2 + core]
        return remote(block, block, ring_ss.at[chunk, number], ring_rs.at[chunk, source_y * 2 + core], device)

    def send_own(chunk):
        ring_copy(chunk, y, along_y(up), 0).start()
        ring_copy(chunk, y, along_y(down), 1).start()
        ring_copy(chunk, y, partner, 2).start()

    def finish(chunk):
        for hop in HOPS:
            two_arrival(chunk, hop).wait_recv()
        me, _ = second_axis(chunk)
        total = residual_ref[:, chunk * 128:(chunk + 1) * 128].astype(F32) + part[chunk, me].astype(F32)
        for hop in HOPS:
            total += came[chunk, (me + hop) % SIDE].astype(F32)
        value = total.astype(BF16)
        stream_ref[:, chunk * 128:(chunk + 1) * 128] = value
        all_[chunk, tensor] = value
        send_own(chunk)

    def finish_last():
        for hop in HOPS:
            two_arrival(3, hop).wait_recv()
        me, _ = second_axis(3)
        kept = residual_ref[:, 384:448].astype(F32)
        total = jnp.concatenate([kept[:64], kept[64:]], axis=1) + part3[me].astype(F32)
        for hop in HOPS:
            total += came3[(me + hop) % SIDE].astype(F32)
        value = total.astype(BF16)
        all3[tensor] = value
        send_own(3)
        wide = value.astype(F32)
        stream_ref[0:64, 384:448] = wide[:, :64].astype(BF16)
        stream_ref[64:128, 384:448] = pltpu.roll(wide, 64, 1)[:, :64].astype(BF16)

    def from_below(chunk, step):
        return (y + SIDE - step) % SIDE

    def from_above(chunk, step):
        return (y + step) % SIDE

    def forward(chunk, step):
        origin = from_below(chunk, step)
        ring_copy(chunk, origin, along_y(up), 0).wait_recv()
        if step < 4:
            ring_copy(chunk, origin, along_y(up), 2 + step).start()
        ring_copy(chunk, origin, partner, 7 + step).start()
        if step < 4:
            origin = from_above(chunk, step)
            ring_copy(chunk, origin, along_y(down), 1).wait_recv()
            if step < 3:
                ring_copy(chunk, origin, along_y(down), 5 + step).start()
            ring_copy(chunk, origin, partner, 11 + step).start()

    def wait_partner(chunk):
        for source in range(SIDE):
            block = buffers(chunk)[4].at[source * 2 + 1 - core]
            remote(block, block, ring_ss.at[chunk, 0], ring_rs.at[chunk, source * 2 + 1 - core], partner).wait_recv()

    def project(chunk):
        wait_partner(chunk)

        def chips(source, carry):
            normed, weights = [], []
            for half in range(2):
                owner = source * 2 + half
                value = all_[chunk, owner].astype(F32)
                square[...] += value * value
                normed.append((value * gain_ref[pl.ds(owner * 4 + chunk, 1), :]).astype(BF16))
                weights.append(proj[pl.ds(pl.multiple_of(owner * COLS + chunk * 128, 16), 128), :])
            acc[...] += jnp.dot(
                jnp.concatenate(normed, axis=1), jnp.concatenate(weights, axis=0), preferred_element_type=F32
            )
            return carry

        lax.fori_loop(0, SIDE, chips, 0)

    def project_last():
        wait_partner(3)

        def chips(source, energy):
            normed, weights = [], []
            for half in range(2):
                owner = source * 2 + half
                value = all3[owner].astype(F32)
                energy = energy + value * value
                scaled = value * gain_ref[pl.ds(owner * 4 + 3, 1), :]
                normed.append(
                    jnp.concatenate([jnp.where(low, scaled, 0.0), jnp.where(low, 0.0, scaled)], axis=0).astype(BF16)
                )
                rows = proj[pl.ds(pl.multiple_of(owner * COLS + 384, 16), 64), :]
                weights += [rows, rows]
            acc[...] += jnp.dot(
                jnp.concatenate(normed, axis=1), jnp.concatenate(weights, axis=0), preferred_element_type=F32
            )
            return energy

        return lax.fori_loop(0, SIDE, chips, jnp.zeros((64, 128), F32))

    acc[...] = jnp.zeros_like(acc)
    square[...] = jnp.zeros_like(square)
    merge(0)
    merge(1)
    merge_last()
    merge(2)
    finish(0)
    load_p.wait()
    for step in range(1, 5):
        forward(0, step)
    finish(1)
    finish(2)
    finish_last()
    for step in range(1, 5):
        for chunk in (1, 2, 3):
            forward(chunk, step)
    for chunk in range(3):
        project(chunk)
    energy3 = project_last()
    energy = jnp.sum(square[...], axis=1, keepdims=True)
    energy += jnp.concatenate(
        [
            jnp.sum(jnp.where(low, energy3, 0.0), axis=1, keepdims=True),
            jnp.sum(jnp.where(low, 0.0, energy3), axis=1, keepdims=True),
        ],
        axis=0,
    )
    latents_ref[...] = (acc[...] * lax.rsqrt(energy / D + epsilon)).astype(BF16)

    for hop in HOPS:
        for copy in meta_copies(hop):
            copy.wait_send()
        for chunk in range(4):
            one_copy(chunk, hop).wait_send()
            two_copy(chunk, hop).wait_send()
    for chunk in range(4):
        for number in (0, 1, 2):
            ring_copy(chunk, y, (along_y(up), along_y(down), partner)[number], number).wait_send()
        for step in range(1, 5):
            origin = from_below(chunk, step)
            if step < 4:
                ring_copy(chunk, origin, along_y(up), 2 + step).wait_send()
            ring_copy(chunk, origin, partner, 7 + step).wait_send()
            if step < 4:
                origin = from_above(chunk, step)
                if step < 3:
                    ring_copy(chunk, origin, along_y(down), 5 + step).wait_send()
                ring_copy(chunk, origin, partner, 11 + step).wait_send()


def on_device(hidden, down_weight, expert_ids, gate_weights, residual, norm_gain, proj_weight):
    meta = jnp.concatenate([expert_ids.astype(F32), gate_weights], axis=1).T
    gain = norm_gain.reshape(16, COLS)
    gain = jnp.concatenate([gain, gain[:, 384:]], axis=1).reshape(64, 128)
    vmem = pl.BlockSpec(memory_space=pltpu.VMEM)
    hbm = pl.BlockSpec(memory_space=pl.ANY)
    dma = pltpu.SemaphoreType.DMA
    wide = (3, SIDE, ROWS, 128)
    return pl.pallas_call(
        kernel,
        name="combine",
        out_shape=(
            jax.ShapeDtypeStruct((TOKENS, COLS), BF16),
            jax.ShapeDtypeStruct((TOKENS, LATENT), BF16),
        ),
        in_specs=[hbm, hbm, hbm, vmem, vmem, vmem],
        out_specs=(vmem, vmem),
        scratch_shapes=[
            pltpu.VMEM((SIDE * ROWS, 2048), BF16),
            pltpu.VMEM((2048, COLS), BF16),
            pltpu.VMEM((2048, 256), BF16),
            pltpu.VMEM((D, LATENT), BF16),
            pltpu.VMEM((SIDE, 16, 128), F32),
            pltpu.VMEM((SIDE, 16, 128), F32),
            pltpu.VMEM((4, 2 * TOKENS, 2 * ROWS), BF16),
            pltpu.VMEM((4, 2 * TOKENS, 2 * ROWS), BF16),
            pltpu.VMEM(wide, BF16),
            pltpu.VMEM((SIDE, ROWS // 2, 128), BF16),
            pltpu.VMEM(wide, BF16),
            pltpu.VMEM((SIDE, ROWS // 2, 128), BF16),
            pltpu.VMEM((3, SIDE, TOKENS, 128), BF16),
            pltpu.VMEM((SIDE, TOKENS // 2, 128), BF16),
            pltpu.VMEM((3, SIDE, TOKENS, 128), BF16),
            pltpu.VMEM((SIDE, TOKENS // 2, 128), BF16),
            pltpu.VMEM((3, 2 * SIDE, TOKENS, 128), BF16),
            pltpu.VMEM((2 * SIDE, TOKENS // 2, 128), BF16),
            pltpu.VMEM((TOKENS, LATENT), F32),
            pltpu.VMEM((TOKENS, 128), F32),
            dma((2,)),
            dma((4,)),
            dma((2, SIDE)),
            dma((2, SIDE)),
            dma((4, SIDE)),
            dma((4, SIDE)),
            dma((4, SIDE)),
            dma((4, SIDE)),
            dma((4, 16)),
            dma((4, 16)),
        ],
        compiler_params=pltpu.CompilerParams(
            collective_id=0, has_side_effects=True, vmem_limit_bytes=56 * 1024 * 1024
        ),
    )(hidden[0], down_weight[0], proj_weight, meta, residual, gain)


def solution(mesh):
    return jax.shard_map(
        on_device,
        mesh=mesh,
        in_specs=(
            P("expert", None, None),
            P("expert", None, "tensor"),
            P("expert", None),
            P("expert", None),
            P("expert", "tensor"),
            P(),
            P(None, "tensor"),
        ),
        out_specs=(P("expert", "tensor"), P("expert", "tensor")),
        check_vma=False,
    )
```
